32 devices in a mesh: group: 2 (over y), seq: 4 (over z), head: 4 (over x, core).
Axes of the slice: x: 2, y: 2, z: 4, core: 2. Of those that a mesh axis runs over, the one named last changes fastest.
Arguments:
- q_lin: bfloat16 [3072, 2048], P(('group', 'seq'), 'head'), parts along dimension 0, may hold values from -6 to 6
- k_lin: bfloat16 [3072, 2048], P(('group', 'seq'), 'head'), parts along dimension 0, may hold values from -6 to 6
- v_lin: bfloat16 [3072, 2048], P(('group', 'seq'), 'head'), parts along dimension 0, may hold values from -6 to 6
- q_soft: bfloat16 [3072, 2048], P(('group', 'seq'), 'head'), parts along dimension 0, may hold values from -5 to 5
- k_soft: bfloat16 [3072, 2048], P(('group', 'seq'), 'head'), parts along dimension 0, may hold values from -5 to 5
- v_soft: bfloat16 [3072, 2048], P(('group', 'seq'), 'head'), parts along dimension 0, may hold values from -6 to 6
- segment: int32 [3072], P(('group', 'seq')), parts along dimension 0, may hold values from 0 to 3, as said below
Outputs:
- mixed_lin: bfloat16 [3072, 2048], P(('group', 'seq'), 'head'), parts along dimension 0
- mixed_soft: bfloat16 [3072, 2048], P(('group', 'seq'), 'head'), parts along dimension 0
The draws below stay inside these ranges and needn't reach their ends.
There are 2 independent parts, one for each index of `group`. The reference program is written for one: setup_inputs(seed, part) draws one part's arguments, and reference() takes and returns one part's arrays. A program takes and returns all parts, laid end to end along the dimension named above; each array names one. Nothing has to cross between parts.
Inputs may be any that keep to these rules, and one draw needn't show every extreme that they name: `segment`: document numbers never fall along the list; each of the 4 documents has 1 to 960 tokens and one has exactly 960.
All inputs are finite; a program needn't handle non-finite values.
Results may differ from the reference program's by a relative error of at most 0.0075.
Values may be sent and summed in bfloat16 or wider, within the bound.
A program may use at most 128 MiB of HBM per device.

```python
import jax
import jax.numpy as jnp
from jax import lax

HEADS = 16
HEAD_DIM = 128
TOK_DEV = 384
NSEG = 4
TOKENS = 1536
SEG_MOST = 960


def drawn_rows(key, which):
    base = jnp.clip(jax.random.normal(jax.random.fold_in(key, which), (TOKENS, HEADS * HEAD_DIM), jnp.float32), -5.0, 5.0)
    return base


def draw_q_soft(key, part):
    return drawn_rows(key, 2).astype(jnp.bfloat16)


def draw_k_soft(key, part):
    return drawn_rows(key, 3).astype(jnp.bfloat16)


def draw_segment(key, part):
    remainder = TOKENS - SEG_MOST
    picks = jax.random.permutation(jax.random.fold_in(key, 5), remainder - 1)[:2] + 1
    cuts = jnp.sort(picks.astype(jnp.int32))
    shorter = jnp.stack([cuts[0], cuts[1] - cuts[0], remainder - cuts[1]]).astype(jnp.int32)
    longest_slot = jax.random.randint(jax.random.fold_in(key, 6), (), 0, NSEG, dtype=jnp.int32)
    slots = jnp.arange(NSEG, dtype=jnp.int32)
    source = jnp.clip(slots - (slots > longest_slot).astype(jnp.int32), 0, 2)
    lengths = jnp.where(slots == longest_slot, jnp.int32(SEG_MOST), shorter[source])
    ends = jnp.cumsum(lengths)[:-1]
    places = jnp.arange(TOKENS, dtype=jnp.int32)
    return jnp.sum((places[:, None] >= ends[None, :]).astype(jnp.int32), axis=1).astype(jnp.int32)


def levels(stream_key, extent, split, smallest, high):
    def one(dim, parts):
        draws = jax.random.uniform(jax.random.fold_in(jax.random.fold_in(stream_key, 6), dim), (parts,), jnp.float32, smallest / len(split), high / len(split))
        return jnp.repeat(jnp.exp(draws), extent[dim] // parts).reshape((-1,) + (1,) * (len(extent) - dim - 1))

    loudness = one(*split[0])
    for cut in split[1:]:
        loudness = loudness * one(*cut)
    return loudness


def normal_values(rng, dims, width, reach, split=(), kind=jnp.bfloat16):
    result = width * jax.random.normal(rng, dims, jnp.float32)
    if split:
        result = result * levels(rng, dims, split, -0.22, 0.18)
    return jnp.clip(result, -reach, reach).astype(kind)


def setup_inputs(seed: int = 0, part: int = 0) -> dict:
    streams_of = jax.random.split(jax.random.key(seed), 8)
    part_splits = jax.random.split(jax.random.fold_in(streams_of[7], part), 8)
    q_lin = normal_values(part_splits[0], (TOKENS, HEADS * HEAD_DIM), 1.0, 6.0, ((0, 4), (1, 4)))
    k_lin = normal_values(part_splits[1], (TOKENS, HEADS * HEAD_DIM), 1.0, 6.0, ((0, 4), (1, 4)))
    v_lin = normal_values(part_splits[2], (TOKENS, HEADS * HEAD_DIM), 1.0, 6.0, ((0, 4), (1, 4)))
    q_soft = draw_q_soft(jax.random.fold_in(jax.random.fold_in(streams_of[7], part), 71), part)
    k_soft = draw_k_soft(jax.random.fold_in(jax.random.fold_in(streams_of[7], part), 71), part)
    v_soft = normal_values(part_splits[5], (TOKENS, HEADS * HEAD_DIM), 1.0, 6.0, ((0, 4), (1, 4)))
    segment = draw_segment(jax.random.fold_in(jax.random.fold_in(streams_of[7], part), 71), part)
    return {"q_lin": q_lin, "k_lin": k_lin, "v_lin": v_lin, "q_soft": q_soft, "k_soft": k_soft, "v_soft": v_soft, "segment": segment}


def linear_layer(q_lin, k_lin, v_lin, segment):
    blocks = q_lin.shape[0] // TOK_DEV
    shape = (blocks, TOK_DEV, HEADS, HEAD_DIM)
    q_all = q_lin.reshape(shape)
    k_all = k_lin.reshape(shape)
    v_all = v_lin.reshape(shape)
    s_all = segment.reshape(blocks, TOK_DEV)
    places = jnp.arange(TOK_DEV, dtype=jnp.int32)

    def step(carry, inputs):
        memory_state, last_id = carry
        query_block_slice, key_block_slice, value_block_slice, s_blk = inputs
        scores = jnp.einsum('thd,shd->hts', query_block_slice, key_block_slice, preferred_element_type=jnp.float32)
        same = (s_blk[:, None] == s_blk[None, :]) & (places[:, None] >= places[None, :])
        scores = jnp.where(same[None], scores, 0.0)
        inner = jnp.einsum('hts,shd->thd', scores, value_block_slice.astype(jnp.float32), precision=lax.Precision.HIGHEST)
        apply = (s_blk.astype(jnp.float32) == last_id).astype(jnp.float32)
        outer_product = jnp.einsum('upi,pis->ups', query_block_slice.astype(jnp.float32), memory_state, precision=lax.Precision.HIGHEST)
        raw = inner + outer_product * apply[:, None, None]
        new_last = s_blk[-1].astype(jnp.float32)
        retain_mask = (s_blk == s_blk[-1]).astype(key_block_slice.dtype)
        local_state = jnp.einsum('piy,piw->iyw', key_block_slice * retain_mask[:, None, None], value_block_slice, preferred_element_type=jnp.float32)
        memory_state = jnp.where(last_id == new_last, memory_state, 0.0) + local_state
        normed = raw * lax.rsqrt(lax.optimization_barrier(jnp.mean(raw * raw, axis=-1, keepdims=True)) + 1e-06)
        return ((memory_state, new_last), normed.astype(jnp.bfloat16))
    start = (jnp.zeros((HEADS, HEAD_DIM, HEAD_DIM), jnp.float32), jnp.float32(-1.0))
    _, outs = lax.scan(step, start, (q_all, k_all, v_all, s_all))
    return outs.reshape(q_lin.shape)

def softmax_layer(q_soft, k_soft, v_soft, segment):
    total_rows = q_soft.shape[0]
    blocks = total_rows // TOK_DEV
    q_heads = q_soft.reshape(blocks, TOK_DEV, HEADS, HEAD_DIM).transpose(2, 0, 1, 3)
    k_heads = k_soft.reshape(total_rows, HEADS, HEAD_DIM).transpose(1, 0, 2)
    v_heads = v_soft.reshape(total_rows, HEADS, HEAD_DIM).transpose(1, 0, 2)
    key_pos = jnp.arange(total_rows, dtype=jnp.int32)
    q_pos_all = key_pos.reshape(blocks, TOK_DEV)
    q_seg_all = segment.reshape(blocks, TOK_DEV)
    scale = HEAD_DIM ** (-0.5)

    def per_head(inputs):
        q_head, k_head, v_head = inputs

        def per_block(block_in):
            query_block_slice, q_pos, q_seg = block_in
            scores = jnp.dot(query_block_slice, k_head.T, preferred_element_type=jnp.float32) * scale
            mask = (key_pos[None, :] <= q_pos[:, None]) & (segment[None, :] == q_seg[:, None])
            top = lax.optimization_barrier(jnp.max(jnp.where(mask, scores, -1e+30), axis=-1, keepdims=True))
            expo = jnp.where(mask, jnp.exp(scores - top), 0.0)
            total = lax.optimization_barrier(jnp.sum(expo, axis=-1, keepdims=True))
            summed = jnp.dot(expo.astype(jnp.bfloat16), v_head, preferred_element_type=jnp.float32)
            return (summed / total).astype(jnp.bfloat16)
        return lax.map(per_block, (q_head, q_pos_all, q_seg_all))
    outs = lax.map(per_head, (q_heads, k_heads, v_heads))
    return outs.transpose(1, 2, 0, 3).reshape(total_rows, HEADS * HEAD_DIM)

def reference(q_lin, k_lin, v_lin, q_soft, k_soft, v_soft, segment):
    mixed_lin = linear_layer(q_lin, k_lin, v_lin, segment)
    mixed_soft = softmax_layer(q_soft, k_soft, v_soft, segment)
    return (mixed_lin, mixed_soft)
```

```python
import functools
import math

import jax
import jax.numpy as jnp
from jax import lax
from jax.experimental import pallas as pl
from jax.experimental.pallas import tpu as pltpu
from jax.sharding import PartitionSpec as P

HEAD_DIM = 128


def entering(shard, axis, combine, identity):
    devices, position = (lax.axis_size(axis), lax.axis_index(axis))
    everything = jax.tree.map(
        lambda part, kind: lax.all_gather(part.astype(kind), axis),
        shard,
        (jnp.bfloat16, jnp.bfloat16),
    )
    start = jax.tree.map(
        lambda part, zero: jnp.broadcast_to(jnp.asarray(zero, part.dtype), part.shape),
        shard,
        identity,
    )

    def hop(k, before):
        reached = k < position
        new = combine(
            before, jax.tree.map(lambda part, own: part[k].astype(own.dtype), everything, shard)
        )
        return jax.tree.map(lambda a, b: jnp.where(reached, a, b), new, before)

    return lax.fori_loop(0, devices, hop, start)


def shifted(value, axis, steps):
    count = lax.axis_size(axis)
    initial, last = (max(0, -steps), min(count, count - steps))
    return lax.ppermute(value, axis, [(source, source + steps) for source in range(initial, last)])


def join_states(earlier, later):
    early_state, early_last = earlier
    late_state, late_last = later
    joined = late_state + jnp.where(early_last == late_last, early_state, 0.0)
    memory_state = jnp.where(late_last < 0.0, early_state, joined)
    last_id = jnp.where(late_last < 0.0, early_last, late_last)
    return (memory_state, last_id)


def on_device(q_lin, k_lin, v_lin, q_soft, k_soft, v_soft, segment):
    rows = q_lin.shape[0]
    heads_here = q_lin.shape[1] // HEAD_DIM
    shape = (rows, heads_here, HEAD_DIM)
    single_query = q_lin.reshape(shape)
    single_key = k_lin.reshape(shape)
    single_value = v_lin.reshape(shape)
    places = jnp.arange(rows, dtype=jnp.int32)
    me_index = lax.axis_index("seq")
    scores = jnp.einsum(
        "thd,shd->hts", single_query, single_key, preferred_element_type=jnp.float32
    )
    same = (segment[:, None] == segment[None, :]) & (places[:, None] >= places[None, :])
    scores = jnp.where(same[None], scores, 0.0)
    inner = jnp.einsum(
        "hts,shd->thd", scores, single_value.astype(jnp.float32), precision=lax.Precision.HIGHEST
    )
    retain_mask = (segment == segment[-1]).astype(single_key.dtype)
    local_state = jnp.einsum(
        "piy,piw->iyw",
        single_key * retain_mask[:, None, None],
        single_value,
        preferred_element_type=jnp.float32,
    )
    own_last = segment[-1].astype(jnp.float32)
    empty = jnp.zeros((heads_here, HEAD_DIM, HEAD_DIM), jnp.float32)
    arriving_state, carried = entering(
        (local_state, own_last), "seq", join_states, (empty, jnp.float32(-1.0))
    )
    apply = (segment.astype(jnp.float32) == carried).astype(jnp.float32)
    outer_product = jnp.einsum(
        "upi,pis->ups",
        single_query.astype(jnp.float32),
        arriving_state,
        precision=lax.Precision.HIGHEST,
    )
    raw = inner + outer_product * apply[:, None, None]
    normed = raw * lax.rsqrt(jnp.mean(raw * raw, axis=-1, keepdims=True) + 1e-06)
    mixed_lin = normed.reshape(rows, heads_here * HEAD_DIM).astype(jnp.bfloat16)
    q_heads = q_soft.reshape(shape)
    q_pos = me_index * rows + places
    scale = HEAD_DIM ** (-0.5)

    def attend(carry, piece, start):
        keys, values, ids = piece
        count = keys.shape[0] // rows
        key_blocks = keys.reshape(count, rows, heads_here, HEAD_DIM)
        value_blocks = values.reshape(count, rows, heads_here, HEAD_DIM)
        id_blocks = ids.reshape(count, rows).astype(jnp.int32)
        offsets = start + rows * jnp.arange(count, dtype=jnp.int32)

        def one_block(memory_state, block_in):
            key_block_slice, value_block_slice, id_blk, offset = block_in
            top, total, accum = memory_state
            logits = (
                jnp.einsum(
                    "thd,shd->hts", q_heads, key_block_slice, preferred_element_type=jnp.float32
                )
                * scale
            )
            key_pos = offset + places
            mask = (
                (key_pos[None, :] <= q_pos[:, None])
                & (key_pos[None, :] >= 0)
                & (id_blk[None, :] == segment[:, None])
            )
            new_top = jnp.maximum(top, jnp.max(jnp.where(mask[None], logits, -1e30), axis=-1))
            factor = jnp.exp(top - new_top)
            expo = jnp.where(mask[None], jnp.exp(logits - new_top[..., None]), 0.0)
            total = total * factor + jnp.sum(expo, axis=-1)
            added = jnp.einsum(
                "hts,shd->thd",
                expo.astype(jnp.bfloat16),
                value_block_slice,
                preferred_element_type=jnp.float32,
            )
            accum = accum * factor.T[:, :, None] + added
            memory_state = (new_top, total, accum)
            return (memory_state, None)

        carry, _ = lax.scan(one_block, carry, (key_blocks, value_blocks, id_blocks, offsets))
        return carry

    start_state = (
        jnp.full((heads_here, rows), -1e30, jnp.float32),
        jnp.zeros((heads_here, rows), jnp.float32),
        jnp.zeros(shape, jnp.float32),
    )
    ids_wire = segment.astype(jnp.bfloat16)
    seq_count = lax.axis_size("seq")
    longest = rows * seq_count * 5 // 8
    reach_steps = min(seq_count - 1, (longest - 2) // rows + 1)
    first_state = attend(start_state, (k_soft, v_soft, ids_wire), me_index * rows)

    def forward(step, loop_carry):
        memory_state, keys, values, ids = loop_carry
        keys, values, ids = shifted((keys, values, ids), "seq", 1)
        memory_state = attend(memory_state, (keys, values, ids), (me_index - step) * rows)
        return (memory_state, keys, values, ids)

    final_carry = lax.fori_loop(
        1, reach_steps + 1, forward, (first_state, k_soft, v_soft, ids_wire)
    )
    top, total, accum = final_carry[0]
    mixed_soft = (
        (accum / total.T[:, :, None]).reshape(rows, heads_here * HEAD_DIM).astype(jnp.bfloat16)
    )
    return (mixed_lin, mixed_soft)


D = HEAD_DIM
BF, F32 = jnp.bfloat16, jnp.float32
OTHER = -65536.0
HIDDEN = -1e30
SCALE2 = D ** (-0.5) * math.log2(math.e)
K_IN, V_IN, Q_A, Q_B, O_A, M_A, O_B, M_B, STATE = range(9)
KINDS = 9


def nt(a, b):
    return lax.dot_general(a, b, (((1,), (1,)), ((), ())), preferred_element_type=F32)


def tn(a, b):
    return lax.dot_general(a, b, (((0,), (0,)), ((), ())), preferred_element_type=F32)


def softmax_part(pieces, query):
    scores = []
    for keys, _, bias in pieces:
        s = nt(keys, query)
        scores.append(s if bias is None else s + bias)
    top = functools.reduce(jnp.maximum, [jnp.max(s, axis=0, keepdims=True) for s in scores])
    total, out = 0.0, 0.0
    for s, (_, values, _) in zip(scores, pieces):
        p = jnp.exp2((s - top) * SCALE2)
        total = total + jnp.sum(p, axis=0, keepdims=True)
        out = out + tn(values, p.astype(BF))
    return top * SCALE2, total, out


def kernel(
    rows, heads, low,
    ql_h, kl_h, vl_h, qs_h, ks_h, vs_h, seg,
    out_l, out_s,
    ql, kl, vl, qs, ks, vs,
    k_in, v_in, q_a, q_b, segs, o_a, m_a, o_b, m_b, state_in,
    o_to_a, m_to_a, o_to_b, m_to_b, state_out,
    bias, e_own, f_own, own_o, own_m, own_l,
    local_sem, seg_send, seg_recv, send_sem, recv_sem,
):
    me = lax.axis_index("seq")
    n = 4
    arrays = ((ql_h, ql), (kl_h, kl), (vl_h, vl), (qs_h, qs), (ks_h, ks), (vs_h, vs))
    loads = [
        pltpu.make_async_copy(a, b, local_sem.at[i]) for i, (a, b) in enumerate(arrays)
    ]
    for load in loads:
        load.start()

    barrier = pltpu.get_barrier_semaphore()
    for step in range(1, n):
        pl.semaphore_signal(
            barrier, inc=1, device_id={"seq": lax.rem(me + step, n)},
            device_id_type=pl.DeviceIdType.MESH,
        )
    pl.semaphore_wait(barrier, n - 1)

    def copy(kind, h, src, dst, to):
        return pltpu.make_async_remote_copy(
            src_ref=src, dst_ref=dst,
            send_sem=send_sem.at[kind, h], recv_sem=recv_sem.at[kind, h],
            device_id={"seq": to}, device_id_type=pl.DeviceIdType.MESH,
        )

    def seg_copy(owner, to):
        return pltpu.make_async_remote_copy(
            src_ref=seg, dst_ref=segs.at[owner],
            send_sem=seg_send.at[to], recv_sem=seg_recv.at[owner],
            device_id={"seq": to}, device_id_type=pl.DeviceIdType.MESH,
        )

    def cols(h):
        return pl.ds(pl.multiple_of(h * D, D), D)

    def each_head(body):
        def run(h, carry):
            body(h)
            return carry
        lax.fori_loop(0, heads, run, 0)

    def column(row):
        return jnp.broadcast_to(row.astype(F32), (D, rows)).T

    lane = lax.broadcasted_iota(jnp.int32, (rows, D), 1).astype(F32)

    def query_side(row):
        return jnp.where(column(row) == lane, 1.0, 0.0).astype(BF)

    def key_side(row):
        return jnp.where(column(row) == lane, 0.0, OTHER).astype(BF)

    def put(ref, h, value):
        ref[:, cols(h)] = value.T.astype(BF)

    def prepare():
        row = seg[...]
        frow = row.astype(F32)
        square = jnp.broadcast_to(frow, (rows, rows))
        s = lax.broadcasted_iota(jnp.int32, (rows, rows), 0)
        t = lax.broadcasted_iota(jnp.int32, (rows, rows), 1)
        bias[...] = jnp.where((s <= t) & (square.T == square), 0.0, HIDDEN)
        e_own[...] = query_side(row)
        f_own[...] = key_side(row)

    def own_keys(h):
        return jnp.concatenate([ks[:, cols(h)], f_own[...]], axis=1)

    def own_query(h):
        return jnp.concatenate([qs[:, cols(h)], e_own[...]], axis=1)

    def linear(h, d):
        k, v, q = kl[:, cols(h)], vl[:, cols(h)], ql[:, cols(h)]
        frow = seg[...].astype(F32)
        if d > 0:
            before = segs[d - 1].astype(F32)[:, rows - 1:]
            copy(STATE, h, state_out.at[h], state_in.at[h], d).wait_recv()
            arrived = state_in[h]
        if d < n - 1:
            kept = (column(seg[...]) == frow[:, rows - 1:]).astype(F32)
            state = tn((v.astype(F32) * kept).astype(BF), k)
            if d > 0:
                state = state + jnp.where(before == frow[:, rows - 1:], arrived.astype(F32), 0.0)
            state_out[h] = state.astype(BF)
            copy(STATE, h, state_out.at[h], state_in.at[h], d + 1).start()
        a = jnp.where(bias[...] == 0.0, nt(k, q), 0.0)
        raw = tn(v, a.astype(BF))
        if d > 0:
            raw = raw + jnp.where(frow == before, nt(arrived, q), 0.0)
        mean = jnp.mean(raw * raw, axis=0, keepdims=True)
        put(out_l, h, raw * lax.rsqrt(mean + 1e-06))

    def keep_own(h):
        m, l, o = softmax_part([(own_keys(h), vs[:, cols(h)], bias[...])], own_query(h))
        own_o[h] = o
        own_m[h] = jnp.broadcast_to(m, (8, rows))
        own_l[h] = jnp.broadcast_to(l, (8, rows))

    def merge(h, others):
        m, l, o = own_m[h][:1], own_l[h][:1], own_o[h]
        sides = [(r_m[h][:1], r_o[h].astype(F32)) for r_o, r_m in others]
        top = functools.reduce(jnp.maximum, [x for x, _ in sides], m)
        w = jnp.exp2(m - top)
        total, out = l * w, o * w
        for x, y in sides:
            w = jnp.exp2(x - top)
            total, out = total + w, out + y * w
        put(out_s, h, out / total)

    def send_part(h, pieces, query, o_ref, m_ref, o_dst, m_dst, o_kind, m_kind, to):
        m, l, o = softmax_part(pieces, query)
        o_ref[h] = (o / l).astype(BF)
        m_ref[h] = jnp.broadcast_to(m + jnp.log(l) * math.log2(math.e), (8, rows))
        copy(o_kind, h, o_ref.at[h], o_dst.at[h], to).start()
        copy(m_kind, h, m_ref.at[h], m_dst.at[h], to).start()

    def load_all():
        for load in loads:
            load.wait()

    @pl.when(me == 0)
    def _():
        seg_copy(0, 1).start()
        for h in range(heads):
            c = slice(h * D, (h + 1) * D)
            copy(K_IN, h, ks_h.at[:, c], k_in.at[:, c], 1).start()
            copy(V_IN, h, vs_h.at[:, c], v_in.at[:, c], 1).start()
        prepare()
        load_all()

        def first(h):
            linear(h, 0)
            m, l, o = softmax_part([(own_keys(h), vs[:, cols(h)], bias[...])], own_query(h))
            put(out_s, h, o / l)

        each_head(first)
        seg_copy(0, 1).wait_send()
        for h in range(heads):
            c = slice(h * D, (h + 1) * D)
            copy(K_IN, h, ks_h.at[:, c], k_in.at[:, c], 1).wait_send()
            copy(V_IN, h, vs_h.at[:, c], v_in.at[:, c], 1).wait_send()
            copy(STATE, h, state_out.at[h], state_in.at[h], 1).wait_send()

    @pl.when(me == 1)
    def _():
        seg_copy(1, 2).start()
        prepare()
        load_all()
        seg_copy(0, 1).wait_recv()
        each_head(lambda h: linear(h, 1))
        for owner in (2, 3):
            seg_copy(owner, 1).wait_recv()
        f_0 = key_side(segs[0])
        e_a, e_b = query_side(segs[2]), query_side(segs[3])

        def middle(h):
            c = cols(h)
            copy(K_IN, h, ks_h.at[:, c], k_in.at[:, c], 1).wait_recv()
            copy(V_IN, h, vs_h.at[:, c], v_in.at[:, c], 1).wait_recv()
            copy(Q_A, h, qs_h.at[:, c], q_a.at[:, c], 1).wait_recv()
            keys = jnp.concatenate([k_in[:, c], f_0], axis=1)
            values = v_in[:, c]
            own = (own_keys(h), vs[:, c], None)
            send_part(
                h, [(keys, values, None), own], jnp.concatenate([q_a[:, c], e_a], axis=1),
                o_to_a, m_to_a, o_a, m_a, O_A, M_A, 2,
            )
            m, l, o = softmax_part(
                [(keys, values, None), (own_keys(h), vs[:, c], bias[...])], own_query(h)
            )
            put(out_s, h, o / l)
            copy(Q_B, h, qs_h.at[:, c], q_b.at[:, c], 1).wait_recv()
            send_part(
                h, [(keys[low:], values[low:], None), own],
                jnp.concatenate([q_b[:, c], e_b], axis=1),
                o_to_b, m_to_b, o_b, m_b, O_B, M_B, 3,
            )

        each_head(middle)
        seg_copy(1, 2).wait_send()
        for h in range(heads):
            copy(STATE, h, state_out.at[h], state_in.at[h], 2).wait_send()
            copy(O_A, h, o_to_a.at[h], o_a.at[h], 2).wait_send()
            copy(M_A, h, m_to_a.at[h], m_a.at[h], 2).wait_send()
            copy(O_B, h, o_to_b.at[h], o_b.at[h], 3).wait_send()
            copy(M_B, h, m_to_b.at[h], m_b.at[h], 3).wait_send()

    @pl.when(me == 2)
    def _():
        seg_copy(2, 1).start()
        seg_copy(2, 3).start()
        for h in range(heads):
            c = slice(h * D, (h + 1) * D)
            copy(Q_A, h, qs_h.at[:, c], q_a.at[:, c], 1).start()
        prepare()
        load_all()
        seg_copy(3, 2).wait_recv()
        e_a = query_side(segs[3])

        def last(h):
            c = cols(h)
            copy(Q_A, h, qs_h.at[:, c], q_a.at[:, c], 2).wait_recv()
            send_part(
                h, [(own_keys(h), vs[:, c], None)], jnp.concatenate([q_a[:, c], e_a], axis=1),
                o_to_a, m_to_a, o_a, m_a, O_A, M_A, 3,
            )

        each_head(last)
        seg_copy(1, 2).wait_recv()
        each_head(lambda h: linear(h, 2))
        each_head(keep_own)

        def finish(h):
            copy(O_A, h, o_to_a.at[h], o_a.at[h], 2).wait_recv()
            copy(M_A, h, m_to_a.at[h], m_a.at[h], 2).wait_recv()
            merge(h, [(o_a, m_a)])

        each_head(finish)
        seg_copy(2, 1).wait_send()
        seg_copy(2, 3).wait_send()
        for h in range(heads):
            c = slice(h * D, (h + 1) * D)
            copy(Q_A, h, qs_h.at[:, c], q_a.at[:, c], 1).wait_send()
            copy(STATE, h, state_out.at[h], state_in.at[h], 3).wait_send()
            copy(O_A, h, o_to_a.at[h], o_a.at[h], 3).wait_send()
            copy(M_A, h, m_to_a.at[h], m_a.at[h], 3).wait_send()

    @pl.when(me == 3)
    def _():
        seg_copy(3, 2).start()
        seg_copy(3, 1).start()
        for kind, dst, to in ((Q_A, q_a, 2), (Q_B, q_b, 1)):
            for h in range(heads):
                c = slice(h * D, (h + 1) * D)
                copy(kind, h, qs_h.at[:, c], dst.at[:, c], to).start()
        prepare()
        load_all()
        each_head(keep_own)
        seg_copy(2, 3).wait_recv()
        each_head(lambda h: linear(h, 3))

        def finish(h):
            copy(O_A, h, o_to_a.at[h], o_a.at[h], 3).wait_recv()
            copy(M_A, h, m_to_a.at[h], m_a.at[h], 3).wait_recv()
            copy(O_B, h, o_to_b.at[h], o_b.at[h], 3).wait_recv()
            copy(M_B, h, m_to_b.at[h], m_b.at[h], 3).wait_recv()
            merge(h, [(o_a, m_a), (o_b, m_b)])

        each_head(finish)
        seg_copy(3, 2).wait_send()
        seg_copy(3, 1).wait_send()
        for kind, dst, to in ((Q_A, q_a, 2), (Q_B, q_b, 1)):
            for h in range(heads):
                c = slice(h * D, (h + 1) * D)
                copy(kind, h, qs_h.at[:, c], dst.at[:, c], to).wait_send()


def four_devices(q_lin, k_lin, v_lin, q_soft, k_soft, v_soft, segment):
    rows, width = q_lin.shape
    heads = width // D
    longest = rows * 4 * 5 // 8
    low = max(0, (3 * rows - longest + 1) // 16 * 16)
    block = pltpu.VMEM((rows, width), BF)
    part = pltpu.VMEM((heads, D, rows), BF)
    stat = pltpu.VMEM((heads, 8, rows), F32)
    state = pltpu.VMEM((heads, D, D), BF)
    out = jax.ShapeDtypeStruct((rows, width), BF)
    vmem = pl.BlockSpec(memory_space=pltpu.VMEM)
    return pl.pallas_call(
        functools.partial(kernel, rows, heads, low),
        out_shape=(out, out),
        in_specs=[pl.BlockSpec(memory_space=pl.ANY)] * 6 + [vmem],
        out_specs=(vmem, vmem),
        scratch_shapes=[block] * 6
        + [block] * 4
        + [pltpu.VMEM((4, 1, rows), jnp.int32), part, stat, part, stat, state]
        + [part, stat, part, stat, state]
        + [
            pltpu.VMEM((rows, rows), F32),
            pltpu.VMEM((rows, D), BF),
            pltpu.VMEM((rows, D), BF),
            pltpu.VMEM((heads, D, rows), F32),
            stat,
            stat,
        ]
        + [
            pltpu.SemaphoreType.DMA((6,)),
            pltpu.SemaphoreType.DMA((4,)),
            pltpu.SemaphoreType.DMA((4,)),
            pltpu.SemaphoreType.DMA((KINDS, heads)),
            pltpu.SemaphoreType.DMA((KINDS, heads)),
        ],
        compiler_params=pltpu.CompilerParams(
            collective_id=0, has_side_effects=True, vmem_limit_bytes=48 * 1024 * 1024
        ),
    )(q_lin, k_lin, v_lin, q_soft, k_soft, v_soft, segment.reshape(1, rows))


def solution(mesh):
    in_specs = (
        P(("group", "seq"), "head"),
        P(("group", "seq"), "head"),
        P(("group", "seq"), "head"),
        P(("group", "seq"), "head"),
        P(("group", "seq"), "head"),
        P(("group", "seq"), "head"),
        P(("group", "seq")),
    )
    out_specs = (P(("group", "seq"), "head"), P(("group", "seq"), "head"))
    return jax.shard_map(
        four_devices if mesh.shape["seq"] == 4 else on_device, mesh=mesh, in_specs=in_specs, out_specs=out_specs, check_vma=False
    )
```
